32 devices in a mesh: lat: 2 (over core), lon: 16 (over z, y, x).
Axes of the slice: x: 2, y: 2, z: 4, core: 2. Of those that a mesh axis runs over, the one named last changes fastest.
Arguments:
- stream: bfloat16 [32, 256, 256], P('lat', 'lon'), may hold values from -6 to 6
- gains: float32 [2, 2, 256], replicated, may hold values from 0.5 to 1.5
- w_qkv: bfloat16 [2, 256, 768], replicated, may hold values from -8 to 8
- table: float32 [2, 4, 13, 7], replicated, may hold values from -4 to 4
- w_out: bfloat16 [2, 256, 256], replicated, may hold values from -0.375 to 0.375
- w_up: bfloat16 [2, 256, 768], replicated, may hold values from -0.375 to 0.375
- kernel: float32 [2, 3, 3, 768], replicated, may hold values from -2 to 2
- w_down: bfloat16 [2, 768, 256], replicated, may hold values from -0.21875 to 0.21875
Outputs:
- result: bfloat16 [32, 256, 256], P('lat', 'lon')
The draws below stay inside these ranges and needn't reach their ends.
All inputs are finite; a program needn't handle non-finite values.
Results may differ from the reference program's by a relative error of at most 0.013.
Values may be sent and summed in bfloat16 or wider, within the bound.
A program may use at most 64 MiB of HBM per device.

```python
import jax
import jax.numpy as jnp
from jax import lax

D = 256
HEADS = 4
FF = 768
WINDOW = 7
LAYERS = 2
CLAT = 16
NLAT = 32
NLON = 256
N_LAT = 2


def draw_w_qkv(key, part):
    spread = D ** (-0.5)
    base = jnp.clip(jax.random.normal(key, (LAYERS, D, 3 * D), jnp.float32) * spread, -4.0 * spread, 4.0 * spread)
    return jnp.clip(base, -8.0, 8.0).astype(jnp.bfloat16)


def block_levels(rng, shape, split, low, high):
    def one(position, blocks):
        draws = jax.random.uniform(jax.random.fold_in(jax.random.fold_in(rng, 6), position), (blocks,), jnp.float32, low / len(split), high / len(split))
        return jnp.repeat(jnp.exp(draws), shape[position] // blocks).reshape((-1,) + (1,) * (len(shape) - position - 1))

    loudness = one(*split[0])
    for cut in split[1:]:
        loudness = loudness * one(*cut)
    return loudness


def bell_draw(own_key, extent, scale, bound, split=(), kind=jnp.bfloat16):
    entries = scale * jax.random.normal(own_key, extent, jnp.float32)
    if split:
        entries = entries * block_levels(own_key, extent, split, -0.22, 0.18)
    return jnp.clip(entries, -bound, bound).astype(kind)


def setup_inputs(seed: int = 0) -> dict:
    streams_of = jax.random.split(jax.random.key(seed), 9)
    stream = bell_draw(streams_of[0], (NLAT, NLON, D), 1.0, 6.0, ((0, 2), (1, 16)))
    gains = jnp.clip(jax.random.uniform(streams_of[1], (LAYERS, 2, D), jnp.float32, 0.5, 1.5), 0.5, 1.5)
    w_qkv = draw_w_qkv(jax.random.fold_in(streams_of[8], 71), 0)
    table = bell_draw(streams_of[3], (LAYERS, HEADS, 2 * WINDOW - 1, WINDOW), 1.0, 4.0, (), jnp.float32)
    w_out = bell_draw(streams_of[4], (LAYERS, D, D), D ** -0.5, 0.375)
    w_up = bell_draw(streams_of[5], (LAYERS, D, FF), D ** -0.5, 0.375)
    kernel = bell_draw(streams_of[6], (LAYERS, 3, 3, FF), 9 ** -0.5, 2.0, (), jnp.float32)
    w_down = bell_draw(streams_of[7], (LAYERS, FF, D), FF ** -0.5, 0.21875)
    return {"stream": stream, "gains": gains, "w_qkv": w_qkv, "table": table, "w_out": w_out, "w_up": w_up, "kernel": kernel, "w_down": w_down}


def rms_normed(wide, gain):
    scale = lax.rsqrt(lax.optimization_barrier(jnp.mean(wide * wide, axis=-1, keepdims=True)) + 1e-06)
    return (wide * scale * gain).astype(jnp.bfloat16)

def make_tiles(source, n_rows, n_cols, side, row_span, col_span, heads, head_size):
    width = source.shape[2]
    source = jnp.pad(source, ((0, (n_rows + 2) * side - source.shape[0]), (0, (n_cols + 1) * side - source.shape[1]), (0, 0)))
    blocks = source.reshape(n_rows + 2, side, (n_cols + 1) * side, width)
    rowed = jnp.concatenate([blocks[:n_rows], blocks[1:n_rows + 1], blocks[2:, :row_span - 2 * side]], axis=1)
    blocks = rowed.reshape(n_rows, row_span, n_cols + 1, side, width)
    both = jnp.concatenate([blocks[:, :, :-1], blocks[:, :, 1:, :col_span - side]], axis=3)
    return both.reshape(n_rows, row_span, n_cols, col_span, heads, head_size)

def neighbour_attention(query, keys, values, first_row, total_rows, bias_table):
    reach = WINDOW // 2
    row_reach = WINDOW - 1
    extra = row_reach - reach
    side = 8
    col_span = side + 2 * reach
    row_span = side + 2 * row_reach
    q_rows, q_cols, width = query.shape
    heads = bias_table.shape[0]
    head_size = width // heads
    n_rows = (q_rows + side - 1) // side
    n_cols = (q_cols + side - 1) // side
    keys = jnp.pad(keys, ((extra, extra), (0, 0), (0, 0)))
    values = jnp.pad(values, ((extra, extra), (0, 0), (0, 0)))
    query = jnp.pad(query, ((0, n_rows * side - q_rows), (0, n_cols * side - q_cols), (0, 0)))
    query_tiles = query.reshape(n_rows, side, n_cols, side, heads, head_size).astype(jnp.float32)
    key_tiles = make_tiles(keys, n_rows, n_cols, side, row_span, col_span, heads, head_size).astype(jnp.float32)
    value_tiles = make_tiles(values, n_rows, n_cols, side, row_span, col_span, heads, head_size).astype(jnp.float32)
    scores = jnp.einsum('aibjhd,apbuhd->abhijpu', query_tiles, key_tiles)
    inner = jnp.arange(side, dtype=jnp.int32)
    outer_rows = jnp.arange(row_span, dtype=jnp.int32)
    outer_cols = jnp.arange(col_span, dtype=jnp.int32)
    row_hot = (outer_rows[None, :, None] - inner[:, None, None] == jnp.arange(2 * WINDOW - 1, dtype=jnp.int32)[None, None, :]).astype(jnp.float32)
    col_hot = (outer_cols[None, :, None] - inner[:, None, None] == jnp.arange(WINDOW, dtype=jnp.int32)[None, None, :]).astype(jnp.float32)
    bias = jnp.einsum('hrc,ipr,juc->hijpu', bias_table, row_hot, col_hot, precision=lax.Precision.HIGHEST)
    tile_rows = first_row + jnp.arange(n_rows, dtype=jnp.int32) * side
    query_rows = tile_rows[:, None] + inner[None, :]
    start = jnp.clip(query_rows - reach, 0, total_rows - WINDOW)
    key_rows = tile_rows[:, None, None] + outer_rows[None, None, :] - row_reach
    row_ok = (key_rows >= start[:, :, None]) & (key_rows < start[:, :, None] + WINDOW)
    offset = outer_cols[None, :] - reach - inner[:, None]
    col_ok = (offset >= -reach) & (offset <= reach)
    allowed = row_ok[:, None, None, :, None, :, None] & col_ok[None, None, None, None, :, None, :]
    scores = scores * head_size ** (-0.5) + bias[None, None]
    scores = jnp.where(allowed, scores, -1000000000.0)
    flat = scores.reshape(n_rows, n_cols, heads, side, side, row_span * col_span)
    peak = lax.optimization_barrier(jnp.max(flat, axis=-1, keepdims=True))
    raised = jnp.exp(flat - peak)
    weights = (raised / lax.optimization_barrier(jnp.sum(raised, axis=-1, keepdims=True))).astype(jnp.bfloat16)
    weights = weights.reshape(n_rows, n_cols, heads, side, side, row_span, col_span).astype(jnp.float32)
    output = jnp.einsum('abhijpu,apbuhd->aibjhd', weights, value_tiles)
    output = output.reshape(n_rows * side, n_cols * side, width)[:q_rows, :q_cols]
    return output.astype(jnp.bfloat16)

def depthwise(padded, weights):
    rows = padded.shape[0] - 2
    cols = padded.shape[1] - 2
    total = jnp.zeros((rows, cols, padded.shape[2]), jnp.float32)
    for first in range(3):
        for second in range(3):
            total = total + weights[first, second] * padded[first:first + rows, second:second + cols].astype(jnp.float32)
    return total

def reference(stream, gains, w_qkv, table, w_out, w_up, kernel, w_down):
    reach = WINDOW // 2
    current = stream
    for layer in range(LAYERS):
        wide = current.astype(jnp.float32)
        normed = rms_normed(wide, gains[layer, 0])
        mixed = jnp.dot(normed, w_qkv[layer], preferred_element_type=jnp.float32).astype(jnp.bfloat16)
        query = mixed[..., :D]
        paired = mixed[..., D:]
        paired = jnp.concatenate([paired[:, -reach:], paired, paired[:, :reach]], axis=1)
        paired = jnp.pad(paired, ((reach, reach), (0, 0), (0, 0)))
        bias_table = table[layer]

        def band(index):
            start = index * CLAT
            band_query = lax.dynamic_slice_in_dim(query, start, CLAT, 0)
            band_pair = lax.dynamic_slice_in_dim(paired, start, CLAT + 2 * reach, 0)
            return neighbour_attention(band_query, band_pair[..., :D], band_pair[..., D:], start, NLAT, bias_table)
        attended = lax.map(band, jnp.arange(N_LAT, dtype=jnp.int32)).reshape(NLAT, NLON, D)
        after = wide + jnp.dot(attended, w_out[layer], preferred_element_type=jnp.float32)
        normed = rms_normed(after, gains[layer, 1])
        lifted = jnp.dot(normed, w_up[layer], preferred_element_type=jnp.float32).astype(jnp.bfloat16)
        lifted = jnp.concatenate([lifted[:, -1:], lifted, lifted[:, :1]], axis=1)
        lifted = jnp.pad(lifted, ((1, 1), (0, 0), (0, 0)))
        hidden = jax.nn.gelu(depthwise(lifted, kernel[layer]), approximate=True).astype(jnp.bfloat16)
        current = (after + jnp.dot(hidden, w_down[layer], preferred_element_type=jnp.float32)).astype(jnp.bfloat16)
    return current
```

```python
import functools

import jax
import jax.numpy as jnp
from jax import lax
from jax.experimental import pallas as pl
from jax.experimental.pallas import tpu as pltpu
from jax.sharding import PartitionSpec as P

WINDOW = 7
REACH = 3
GROUP = 4
F32 = jnp.float32
BF16 = jnp.bfloat16

LEFT, RIGHT, TOP, BOTTOM, TOP_L, TOP_R, BOT_L, BOT_R = range(8)
STEPS = ((0, 1), (0, -1), (1, 0), (-1, 0), (1, 1), (1, -1), (-1, 1), (-1, -1))


def iota(shape, dim):
    return lax.broadcasted_iota(jnp.int32, shape, dim)


def hot(cond):
    return jnp.where(cond, 1.0, 0.0).astype(BF16)


def dot(a, b):
    return jnp.dot(a, b, preferred_element_type=F32)


def normed(wide, gain):
    scale = lax.rsqrt(jnp.mean(wide * wide, axis=-1, keepdims=True) + 1e-06)
    return (wide * scale * gain).astype(BF16)


def kernel(
    n_lat, n_lon, x_ref, gains_ref, table_ref, conv_ref, wqkv_hbm, wout_hbm, wup_hbm, wdown_hbm,
    out_ref, wqkv, wout, wup, wdown, kvb, left, right, edge, lifted, ledge, halo, lpad, pre, flat,
    bias, attn, w_sem, send_sem, recv_sem,
):
    layers = wqkv.shape[0]
    tokens, width = x_ref.shape
    cols = 16
    heads = table_ref.shape[0] // layers
    hid = wup.shape[2]
    lat = lax.axis_index("lat")
    lon = lax.axis_index("lon")
    has_up = lat > 0
    has_down = lat < n_lat - 1
    total_rows = n_lat * (tokens // cols)
    first_row = lat * (tokens // cols)

    loads = {}
    for n in range(layers):
        pairs = ((wqkv_hbm, wqkv), (wout_hbm, wout), (wup_hbm, wup), (wdown_hbm, wdown))
        for k, (src, dst) in enumerate(pairs):
            loads[n, k] = pltpu.make_async_copy(src.at[n], dst.at[n], w_sem.at[n, k])
            loads[n, k].start()

    def target(step):
        return {"lat": lat + step[0], "lon": lax.rem(lon + step[1] + n_lon, n_lon)}

    def when_to(step, go):
        if step[0] == 0:
            go()
        else:
            pl.when(has_down if step[0] > 0 else has_up)(go)

    def when_from(step, go):
        when_to((-step[0], -step[1]), go)

    barrier = pltpu.get_barrier_semaphore()
    for step in STEPS:
        when_to(
            step,
            lambda step=step: pl.semaphore_signal(
                barrier, inc=1, device_id=target(step), device_id_type=pl.DeviceIdType.MESH
            ),
        )

    def messages(n, which):
        if which == 0:
            kv, lo, ro, ed = kvb.at[n], left.at[n], right.at[n], edge.at[n]
            return (
                (ed.at[pl.ds(64, 64)], lo.at[pl.ds(16, 64)]),
                (ed.at[pl.ds(0, 64)], ro.at[pl.ds(16, 64)]),
                (kv.at[pl.ds(256, 48)], kv.at[pl.ds(0, 48)]),
                (kv.at[pl.ds(48, 48)], kv.at[pl.ds(304, 48)]),
                (ed.at[pl.ds(112, 16)], lo.at[pl.ds(0, 16)]),
                (ed.at[pl.ds(48, 16)], ro.at[pl.ds(0, 16)]),
                (ed.at[pl.ds(64, 16)], lo.at[pl.ds(80, 16)]),
                (ed.at[pl.ds(0, 16)], ro.at[pl.ds(80, 16)]),
            )
        low, high = lifted.at[n, pl.ds(0, 16)], lifted.at[n, pl.ds(240, 16)]
        sources = (
            ledge.at[n, pl.ds(16, 16)], ledge.at[n, pl.ds(0, 16)], high, low, high, high, low, low,
        )
        return tuple((src, halo.at[n, slot]) for slot, src in enumerate(sources))

    def remote(n, which, slot):
        src, dst = messages(n, which)[slot]
        return pltpu.make_async_remote_copy(
            src_ref=src,
            dst_ref=dst,
            send_sem=send_sem.at[2 * n + which, slot],
            recv_sem=recv_sem.at[2 * n + which, slot],
            device_id=target(STEPS[slot]),
            device_id_type=pl.DeviceIdType.MESH,
        )

    def send(n, which):
        for slot, step in enumerate(STEPS):
            when_to(step, lambda slot=slot: remote(n, which, slot).start())

    def receive(n, which):
        for slot, step in enumerate(STEPS):
            when_from(step, lambda slot=slot: remote(n, which, slot).wait_recv())

    @pl.when(jnp.logical_not(has_up))
    def _():
        for n in range(layers):
            kvb[n, 0:48] = jnp.zeros((48, 2 * width), BF16)
            left[n, 0:16] = jnp.zeros((16, 2 * width), BF16)
            right[n, 0:16] = jnp.zeros((16, 2 * width), BF16)
            for slot in (TOP, TOP_L, TOP_R):
                halo[n, slot] = jnp.zeros((16, hid), BF16)

    @pl.when(jnp.logical_not(has_down))
    def _():
        for n in range(layers):
            kvb[n, 304:352] = jnp.zeros((48, 2 * width), BF16)
            left[n, 80:96] = jnp.zeros((16, 2 * width), BF16)
            right[n, 80:96] = jnp.zeros((16, 2 * width), BF16)
            for slot in (BOTTOM, BOT_L, BOT_R):
                halo[n, slot] = jnp.zeros((16, hid), BF16)

    lpad[0:16] = jnp.zeros((16, hid), F32)
    lpad[272:288] = jnp.zeros((16, hid), F32)

    m, t = iota((128, tokens), 0), iota((128, tokens), 1)
    pick_kv = hot(t == ((m & 63) >> 2) * cols + (m & 3) + jnp.where(m >= 64, cols - 4, 0))
    m, t = iota((32, tokens), 0), iota((32, tokens), 1)
    pick_lift = hot(t == (m & 15) * cols + jnp.where(m >= 16, cols - 1, 0))
    t, k = iota((tokens, 64), 0), iota((tokens, 64), 1)
    place = hot(((k & 15) == (t >> 4)) & ((t & 15) == jnp.where(k < 32, 0, cols - 1)))
    head_of = iota((1, width), 1) >> 6
    head_hot = [hot(head_of == h) for h in range(heads)]

    def build_bias():
        flat[...] = jnp.zeros_like(flat)
        for a in range(2 * WINDOW - 1):
            row = table_ref[:, a, :]
            flat[0, :, 16 * a : 16 * a + 7] = row
            flat[1, :, 4 * a : 4 * a + 3] = row[:, 0:3]
            flat[2, :, 4 * a : 4 * a + 4] = row[:, 3:7]
        x = iota((16, 256), 1)
        j = iota((16, 256), 0)
        own = x < 160
        on_left = x < 208
        y = jnp.where(on_left, x - 160, x - 208)
        p = jnp.where(own, x >> 4, (y >> 2) - 1)
        c = jnp.where(own, x & 15, jnp.where(on_left, (y & 3) - 4, (y & 3) + cols))
        col_ok = (c - j >= -REACH) & (c - j <= REACH)
        for i in range(GROUP):
            oks = []
            for group in (0, 1, 3):
                g = first_row + GROUP * group + i
                start = jnp.clip(g - REACH, 0, total_rows - WINDOW)
                r = first_row + GROUP * group - REACH + p
                oks.append(col_ok & (r >= start) & (r < start + WINDOW))
            for n in range(layers):
                for h in range(heads):
                    row = n * heads + h

                    def turned(which, shift):
                        base = pltpu.roll(flat[which, row : row + 1, :], shift % 256, 1)
                        base = jnp.broadcast_to(base, (16, 256))
                        return pltpu.roll(base, 0, 1, stride=1, stride_axis=0)

                    value = jnp.where(
                        own,
                        turned(0, 16 * i - 51),
                        jnp.where(
                            on_left, turned(1, 160 + 4 * i - 7), turned(2, 208 + 4 * i - 24)
                        ),
                    )
                    at = h * 64 + i * 16
                    for var in range(3):
                        bias[n, var, at : at + 16, :] = jnp.where(oks[var], value, -1000000000.0)

    wide = x_ref[...].astype(F32)
    for n in range(layers):
        norm = normed(wide, gains_ref[n, 0:1, :])
        loads[n, 0].wait()
        kv = dot(norm, wqkv[n, :, width:]).astype(BF16)
        kvb[n, 48:304] = kv
        edge[n] = dot(pick_kv, kv).astype(BF16)
        if n == 0:
            count = 2 + jnp.where(has_up, 3, 0) + jnp.where(has_down, 3, 0)
            pl.semaphore_wait(barrier, count)
        send(n, 0)
        query = (dot(norm, wqkv[n, :, :width]).astype(BF16) * (width // heads) ** (-0.5)).astype(BF16)
        if n == 0:
            build_bias()
        receive(n, 0)
        for group in range(4):
            parts = [
                kvb[n, 64 * group : 64 * group + 160, :],
                left[n, 16 * group : 16 * group + 48, :],
                right[n, 16 * group : 16 * group + 48, :],
            ]
            near = jnp.concatenate(parts, axis=0)
            q = query[64 * group : 64 * group + 64, :]
            stacked = jnp.concatenate([q * head_hot[h] for h in range(heads)], axis=0)
            scores = lax.dot_general(
                stacked, near[:, :width], (((1,), (1,)), ((), ())), preferred_element_type=F32
            )
            scores = scores + bias[n, (0, 1, 1, 2)[group]]
            raised = jnp.exp(scores - jnp.max(scores, axis=-1, keepdims=True))
            weights = (raised * (1.0 / jnp.sum(raised, axis=-1, keepdims=True))).astype(BF16)
            mixed = dot(weights, near[:, width:])
            total = jnp.where(head_of == 0, mixed[0:64], 0.0)
            for h in range(1, heads):
                total = jnp.where(head_of == h, mixed[64 * h : 64 * h + 64], total)
            attn[64 * group : 64 * group + 64, :] = total.astype(BF16)
        loads[n, 1].wait()
        after = wide + dot(attn[...], wout[n])
        norm = normed(after, gains_ref[n, 1:2, :])
        loads[n, 2].wait()
        lift = dot(norm, wup[n]).astype(BF16)
        lifted[n] = lift
        ledge[n] = dot(pick_lift, lift).astype(BF16)
        send(n, 1)
        lpad[16:272] = lift.astype(F32)
        col = iota((tokens, 128), 0) & 15
        for ch in range(hid // 128):
            at = slice(128 * ch, 128 * ch + 128)
            above, here, below = lpad[0:256, at], lpad[16:272, at], lpad[32:288, at]

            def column(b):
                return (
                    conv_ref[n, 0, b : b + 1, at] * above
                    + conv_ref[n, 1, b : b + 1, at] * here
                    + conv_ref[n, 2, b : b + 1, at] * below
                )

            pre[:, at] = (
                column(1)
                + jnp.where(col > 0, pltpu.roll(column(0), 1, 0), 0.0)
                + jnp.where(col < cols - 1, pltpu.roll(column(2), tokens - 1, 0), 0.0)
            )
        receive(n, 1)
        line = iota((16, hid), 0)
        got = [halo[n, slot].astype(F32) for slot in range(8)]

        def tap(a, b):
            return conv_ref[n, a, b : b + 1, :]

        def row_part(a, middle, at_left, at_right):
            back = jnp.where(line == 0, pltpu.roll(at_left, 1, 0), pltpu.roll(middle, 1, 0))
            ahead = jnp.where(line == 15, pltpu.roll(at_right, 15, 0), pltpu.roll(middle, 15, 0))
            return tap(a, 0) * back + tap(a, 1) * middle + tap(a, 2) * ahead

        def col_part(b, values):
            up = jnp.where(line == 0, 0.0, pltpu.roll(values, 1, 0))
            down = jnp.where(line == 15, 0.0, pltpu.roll(values, 15, 0))
            return tap(0, b) * up + tap(1, b) * values + tap(2, b) * down

        pieces = []
        for part in (col_part(0, got[LEFT]), col_part(2, got[RIGHT])):
            high = part.astype(BF16)
            pieces += [high, (part - high.astype(F32)).astype(BF16)]
        pre[0:16] += row_part(0, got[TOP], got[TOP_L], got[TOP_R])
        pre[240:256] += row_part(2, got[BOTTOM], got[BOT_L], got[BOT_R])
        whole = pre[...] + dot(place, jnp.concatenate(pieces, axis=0))
        hidden = jax.nn.gelu(whole, approximate=True).astype(BF16)
        loads[n, 3].wait()
        result = (after + dot(hidden, wdown[n])).astype(BF16)
        if n == layers - 1:
            out_ref[...] = result
        wide = result.astype(F32)

    for n in range(layers):
        for which in range(2):
            for slot, step in enumerate(STEPS):
                when_to(step, lambda slot=slot: remote(n, which, slot).wait_send())


def on_device(n_lat, n_lon, stream, gains, w_qkv, table, w_out, w_up, conv, w_down):
    rows, cols, width = stream.shape
    layers, heads = table.shape[:2]
    hid = w_up.shape[2]
    vmem = pl.BlockSpec(memory_space=pltpu.VMEM)
    anywhere = pl.BlockSpec(memory_space=pl.ANY)
    result = pl.pallas_call(
        functools.partial(kernel, n_lat, n_lon),
        out_shape=jax.ShapeDtypeStruct((rows * cols, width), BF16),
        in_specs=[vmem] * 4 + [anywhere] * 4,
        out_specs=vmem,
        scratch_shapes=[
            pltpu.VMEM(w_qkv.shape, BF16),
            pltpu.VMEM(w_out.shape, BF16),
            pltpu.VMEM(w_up.shape, BF16),
            pltpu.VMEM(w_down.shape, BF16),
            pltpu.VMEM((layers, 352, 2 * width), BF16),
            pltpu.VMEM((layers, 96, 2 * width), BF16),
            pltpu.VMEM((layers, 96, 2 * width), BF16),
            pltpu.VMEM((layers, 128, 2 * width), BF16),
            pltpu.VMEM((layers, 256, hid), BF16),
            pltpu.VMEM((layers, 32, hid), BF16),
            pltpu.VMEM((layers, 8, 16, hid), BF16),
            pltpu.VMEM((288, hid), F32),
            pltpu.VMEM((256, hid), F32),
            pltpu.VMEM((3, layers * heads, 256), F32),
            pltpu.VMEM((layers, 3, 256, 256), F32),
            pltpu.VMEM((256, width), BF16),
            pltpu.SemaphoreType.DMA((layers, 4)),
            pltpu.SemaphoreType.DMA((2 * layers, 8)),
            pltpu.SemaphoreType.DMA((2 * layers, 8)),
        ],
        compiler_params=pltpu.CompilerParams(
            collective_id=0, has_side_effects=True, vmem_limit_bytes=48 * 1024 * 1024
        ),
    )(
        stream.reshape(rows * cols, width),
        gains,
        table.reshape(layers * heads, *table.shape[2:]),
        conv,
        w_qkv,
        w_out,
        w_up,
        w_down,
    )
    return result.reshape(rows, cols, width)


def solution(mesh):
    sizes = dict(mesh.shape)
    in_specs = (P("lat", "lon", None), P(), P(), P(), P(), P(), P(), P())
    return jax.shard_map(
        functools.partial(on_device, sizes["lat"], sizes["lon"]),
        mesh=mesh,
        in_specs=in_specs,
        out_specs=P("lat", "lon", None),
        check_vma=False,
    )
```

```python
import functools

import jax
import jax.numpy as jnp
from jax import lax
from jax.experimental import pallas as pl
from jax.experimental.pallas import tpu as pltpu
from jax.sharding import PartitionSpec as P

WINDOW = 7
REACH = 3
GROUP = 4
F32 = jnp.float32
BF16 = jnp.bfloat16

LEFT, RIGHT, TOP, BOTTOM, TOP_L, TOP_R, BOT_L, BOT_R = range(8)
STEPS = ((0, 1), (0, -1), (1, 0), (-1, 0), (1, 1), (1, -1), (-1, 1), (-1, -1))


def iota(shape, dim):
    return lax.broadcasted_iota(jnp.int32, shape, dim)


def hot(cond):
    return jnp.where(cond, 1.0, 0.0).astype(BF16)


def dot(a, b):
    return jnp.dot(a, b, preferred_element_type=F32)


def normed(wide, gain):
    scale = lax.rsqrt(jnp.mean(wide * wide, axis=-1, keepdims=True) + 1e-06)
    return (wide * scale * gain).astype(BF16)


def kernel(
    n_lat, n_lon, x_hbm, gains_hbm, table_hbm, conv_hbm, wqkv_hbm, wout_hbm, wup_hbm, wdown_hbm,
    out_ref, x_ref, gains_ref, table, conv_ref, wqkv, wout, wup, wdown, kvb, left, right, edge, lifted, ledge, halo, lpad, pre, rows, spread,
    bias, attn, in_sem, w_sem, send_sem, recv_sem,
):
    layers = wqkv.shape[0]
    tokens, width = x_ref.shape
    cols = 16
    heads = table.shape[2]
    hid = wup.shape[2]
    lat = lax.axis_index("lat")
    lon = lax.axis_index("lon")
    has_up = lat > 0
    has_down = lat < n_lat - 1
    total_rows = n_lat * (tokens // cols)
    first_row = lat * (tokens // cols)

    loads = {}
    firsts = (("x", x_hbm, x_ref), ("gains", gains_hbm, gains_ref), ("table", table_hbm, table), ("conv", conv_hbm, conv_ref))
    for k, (name, src, dst) in enumerate(firsts):
        loads[name] = pltpu.make_async_copy(src, dst, in_sem.at[k])
    loads["x"].start()
    loads["gains"].start()
    for n in range(layers):
        pairs = ((wqkv_hbm, wqkv), (wout_hbm, wout), (wup_hbm, wup), (wdown_hbm, wdown))
        for k, (src, dst) in enumerate(pairs):
            loads[n, k] = pltpu.make_async_copy(src.at[n], dst.at[n], w_sem.at[n, k])
            loads[n, k].start()
            if n == 0 and k == 0:
                loads["table"].start()
                loads["conv"].start()

    def target(step):
        return {"lat": lat + step[0], "lon": lax.rem(lon + step[1] + n_lon, n_lon)}

    def when_to(step, go):
        if step[0] == 0:
            go()
        else:
            pl.when(has_down if step[0] > 0 else has_up)(go)

    def when_from(step, go):
        when_to((-step[0], -step[1]), go)

    barrier = pltpu.get_barrier_semaphore()
    for step in STEPS:
        when_to(
            step,
            lambda step=step: pl.semaphore_signal(
                barrier, inc=1, device_id=target(step), device_id_type=pl.DeviceIdType.MESH
            ),
        )

    def messages(n, which):
        if which == 0:
            kv, lo, ro, ed = kvb.at[n], left.at[n], right.at[n], edge.at[n]
            return (
                (ed.at[pl.ds(64, 64)], lo.at[pl.ds(16, 64)]),
                (ed.at[pl.ds(0, 64)], ro.at[pl.ds(16, 64)]),
                (kv.at[pl.ds(256, 48)], kv.at[pl.ds(0, 48)]),
                (kv.at[pl.ds(48, 48)], kv.at[pl.ds(304, 48)]),
                (ed.at[pl.ds(112, 16)], lo.at[pl.ds(0, 16)]),
                (ed.at[pl.ds(48, 16)], ro.at[pl.ds(0, 16)]),
                (ed.at[pl.ds(64, 16)], lo.at[pl.ds(80, 16)]),
                (ed.at[pl.ds(0, 16)], ro.at[pl.ds(80, 16)]),
            )
        low, high = lifted.at[n, pl.ds(0, 16)], lifted.at[n, pl.ds(240, 16)]
        sources = (
            ledge.at[n, pl.ds(16, 16)], ledge.at[n, pl.ds(0, 16)], high, low, high, high, low, low,
        )
        return tuple((src, halo.at[n, slot]) for slot, src in enumerate(sources))

    def remote(n, which, slot):
        src, dst = messages(n, which)[slot]
        return pltpu.make_async_remote_copy(
            src_ref=src,
            dst_ref=dst,
            send_sem=send_sem.at[2 * n + which, slot],
            recv_sem=recv_sem.at[2 * n + which, slot],
            device_id=target(STEPS[slot]),
            device_id_type=pl.DeviceIdType.MESH,
        )

    def send(n, which):
        for slot, step in enumerate(STEPS):
            when_to(step, lambda slot=slot: remote(n, which, slot).start())

    def receive(n, which):
        for slot, step in enumerate(STEPS):
            when_from(step, lambda slot=slot: remote(n, which, slot).wait_recv())

    @pl.when(jnp.logical_not(has_up))
    def _():
        for n in range(layers):
            kvb[n, 0:48] = jnp.zeros((48, 2 * width), BF16)
            left[n, 0:16] = jnp.zeros((16, 2 * width), BF16)
            right[n, 0:16] = jnp.zeros((16, 2 * width), BF16)
            for slot in (TOP, TOP_L, TOP_R):
                halo[n, slot] = jnp.zeros((16, hid), BF16)

    @pl.when(jnp.logical_not(has_down))
    def _():
        for n in range(layers):
            kvb[n, 304:352] = jnp.zeros((48, 2 * width), BF16)
            left[n, 80:96] = jnp.zeros((16, 2 * width), BF16)
            right[n, 80:96] = jnp.zeros((16, 2 * width), BF16)
            for slot in (BOTTOM, BOT_L, BOT_R):
                halo[n, slot] = jnp.zeros((16, hid), BF16)

    lpad[0:16] = jnp.zeros((16, hid), F32)
    lpad[272:288] = jnp.zeros((16, hid), F32)

    m, t = iota((128, tokens), 0), iota((128, tokens), 1)
    pick_kv = hot(t == ((m & 63) >> 2) * cols + (m & 3) + jnp.where(m >= 64, cols - 4, 0))
    m, t = iota((32, tokens), 0), iota((32, tokens), 1)
    pick_lift = hot(t == (m & 15) * cols + jnp.where(m >= 16, cols - 1, 0))
    t, k = iota((tokens, 64), 0), iota((tokens, 64), 1)
    place = hot(((k & 15) == (t >> 4)) & ((t & 15) == jnp.where(k < 32, 0, cols - 1)))
    head_of = iota((1, width), 1) >> 6
    head_hot = [hot(head_of == h) for h in range(heads)]

    def build_bias():
        for n in range(layers):
            for b in range(WINDOW):
                rows[b, heads * n : heads * (n + 1), 0 : 2 * WINDOW - 1] = table[n, b]
        x = iota((16, 256), 1)
        j = iota((16, 256), 0)
        own = x < 160
        on_left = x < 208
        y = jnp.where(on_left, x - 160, x - 208)
        p = jnp.where(own, x >> 4, (y >> 2) - 1)
        c = jnp.where(own, x & 15, jnp.where(on_left, (y & 3) - 4, (y & 3) + cols))
        col_ok = (c - j >= -REACH) & (c - j <= REACH)
        for i in range(GROUP):
            oks = []
            for group in (0, 1, 3):
                g = first_row + GROUP * group + i
                start = jnp.clip(g - REACH, 0, total_rows - WINDOW)
                r = first_row + GROUP * group - REACH + p
                oks.append(col_ok & (r >= start) & (r < start + WINDOW))
            for half in range(2):
                at = slice(128 * half, 128 * half + 128)
                pick = jnp.clip(p[0:8, at] - i + REACH, 0, 2 * WINDOW - 2)
                for b in range(WINDOW):
                    spread[b, :, at] = jnp.take_along_axis(rows[b], pick, axis=1)
            for n in range(layers):
                for h in range(heads):
                    row = n * heads + h
                    value = jnp.broadcast_to(spread[0, row : row + 1, :], (16, 256))
                    for b in range(1, WINDOW):
                        value = jnp.where(c - j == b - REACH, spread[b, row : row + 1, :], value)
                    at = h * 64 + i * 16
                    for var in range(3):
                        bias[n, var, at : at + 16, :] = jnp.where(oks[var], value, -1000000000.0)

    loads["x"].wait()
    loads["gains"].wait()
    wide = x_ref[...].astype(F32)
    for n in range(layers):
        norm = normed(wide, gains_ref[n, 0:1, :])
        loads[n, 0].wait()
        kv = dot(norm, wqkv[n, :, width:]).astype(BF16)
        kvb[n, 48:304] = kv
        edge[n] = dot(pick_kv, kv).astype(BF16)
        if n == 0:
            count = 2 + jnp.where(has_up, 3, 0) + jnp.where(has_down, 3, 0)
            pl.semaphore_wait(barrier, count)
        send(n, 0)
        query = (dot(norm, wqkv[n, :, :width]).astype(BF16) * (width // heads) ** (-0.5)).astype(BF16)
        if n == 0:
            loads["table"].wait()
            build_bias()
            loads["conv"].wait()
        receive(n, 0)
        for group in range(4):
            parts = [
                kvb[n, 64 * group : 64 * group + 160, :],
                left[n, 16 * group : 16 * group + 48, :],
                right[n, 16 * group : 16 * group + 48, :],
            ]
            near = jnp.concatenate(parts, axis=0)
            q = query[64 * group : 64 * group + 64, :]
            stacked = jnp.concatenate([q * head_hot[h] for h in range(heads)], axis=0)
            scores = lax.dot_general(
                stacked, near[:, :width], (((1,), (1,)), ((), ())), preferred_element_type=F32
            )
            scores = scores + bias[n, (0, 1, 1, 2)[group]]
            raised = jnp.exp(scores - jnp.max(scores, axis=-1, keepdims=True))
            weights = (raised * (1.0 / jnp.sum(raised, axis=-1, keepdims=True))).astype(BF16)
            mixed = dot(weights, near[:, width:])
            total = jnp.where(head_of == 0, mixed[0:64], 0.0)
            for h in range(1, heads):
                total = jnp.where(head_of == h, mixed[64 * h : 64 * h + 64], total)
            attn[64 * group : 64 * group + 64, :] = total.astype(BF16)
        loads[n, 1].wait()
        after = wide + dot(attn[...], wout[n])
        norm = normed(after, gains_ref[n, 1:2, :])
        loads[n, 2].wait()
        lift = dot(norm, wup[n]).astype(BF16)
        lifted[n] = lift
        ledge[n] = dot(pick_lift, lift).astype(BF16)
        send(n, 1)
        lpad[16:272] = lift.astype(F32)
        col = iota((tokens, 128), 0) & 15
        for ch in range(hid // 128):
            at = slice(128 * ch, 128 * ch + 128)
            above, here, below = lpad[0:256, at], lpad[16:272, at], lpad[32:288, at]

            def column(b):
                return (
                    conv_ref[0, b, n : n + 1, at] * above
                    + conv_ref[1, b, n : n + 1, at] * here
                    + conv_ref[2, b, n : n + 1, at] * below
                )

            pre[:, at] = (
                column(1)
                + jnp.where(col > 0, pltpu.roll(column(0), 1, 0), 0.0)
                + jnp.where(col < cols - 1, pltpu.roll(column(2), tokens - 1, 0), 0.0)
            )
        receive(n, 1)
        line = iota((16, hid), 0)
        got = [halo[n, slot].astype(F32) for slot in range(8)]

        def tap(a, b):
            return conv_ref[a, b, n : n + 1, :]

        def row_part(a, middle, at_left, at_right):
            back = jnp.where(line == 0, pltpu.roll(at_left, 1, 0), pltpu.roll(middle, 1, 0))
            ahead = jnp.where(line == 15, pltpu.roll(at_right, 15, 0), pltpu.roll(middle, 15, 0))
            return tap(a, 0) * back + tap(a, 1) * middle + tap(a, 2) * ahead

        def col_part(b, values):
            up = jnp.where(line == 0, 0.0, pltpu.roll(values, 1, 0))
            down = jnp.where(line == 15, 0.0, pltpu.roll(values, 15, 0))
            return tap(0, b) * up + tap(1, b) * values + tap(2, b) * down

        pieces = []
        for part in (col_part(0, got[LEFT]), col_part(2, got[RIGHT])):
            high = part.astype(BF16)
            pieces += [high, (part - high.astype(F32)).astype(BF16)]
        pre[0:16] += row_part(0, got[TOP], got[TOP_L], got[TOP_R])
        pre[240:256] += row_part(2, got[BOTTOM], got[BOT_L], got[BOT_R])
        whole = pre[...] + dot(place, jnp.concatenate(pieces, axis=0))
        hidden = jax.nn.gelu(whole, approximate=True).astype(BF16)
        loads[n, 3].wait()
        result = (after + dot(hidden, wdown[n])).astype(BF16)
        if n == layers - 1:
            out_ref[...] = result
        wide = result.astype(F32)

    for n in range(layers):
        for which in range(2):
            for slot, step in enumerate(STEPS):
                when_to(step, lambda slot=slot: remote(n, which, slot).wait_send())


def on_device(n_lat, n_lon, stream, gains, w_qkv, table, w_out, w_up, conv, w_down):
    rows, cols, width = stream.shape
    layers, heads = table.shape[:2]
    table = table.transpose(0, 3, 1, 2)
    conv = conv.transpose(1, 2, 0, 3)
    hid = w_up.shape[2]
    vmem = pl.BlockSpec(memory_space=pltpu.VMEM)
    anywhere = pl.BlockSpec(memory_space=pltpu.HBM)
    result = pl.pallas_call(
        functools.partial(kernel, n_lat, n_lon),
        out_shape=jax.ShapeDtypeStruct((rows * cols, width), BF16),
        in_specs=[anywhere] * 8,
        out_specs=vmem,
        scratch_shapes=[
            pltpu.VMEM((rows * cols, width), BF16),
            pltpu.VMEM(gains.shape, F32),
            pltpu.VMEM(table.shape, F32),
            pltpu.VMEM(conv.shape, F32),
            pltpu.VMEM(w_qkv.shape, BF16),
            pltpu.VMEM(w_out.shape, BF16),
            pltpu.VMEM(w_up.shape, BF16),
            pltpu.VMEM(w_down.shape, BF16),
            pltpu.VMEM((layers, 352, 2 * width), BF16),
            pltpu.VMEM((layers, 96, 2 * width), BF16),
            pltpu.VMEM((layers, 96, 2 * width), BF16),
            pltpu.VMEM((layers, 128, 2 * width), BF16),
            pltpu.VMEM((layers, 256, hid), BF16),
            pltpu.VMEM((layers, 32, hid), BF16),
            pltpu.VMEM((layers, 8, 16, hid), BF16),
            pltpu.VMEM((288, hid), F32),
            pltpu.VMEM((256, hid), F32),
            pltpu.VMEM((WINDOW, layers * heads, 128), F32),
            pltpu.VMEM((WINDOW, layers * heads, 256), F32),
            pltpu.VMEM((layers, 3, 256, 256), F32),
            pltpu.VMEM((256, width), BF16),
            pltpu.SemaphoreType.DMA((4,)),
            pltpu.SemaphoreType.DMA((layers, 4)),
            pltpu.SemaphoreType.DMA((2 * layers, 8)),
            pltpu.SemaphoreType.DMA((2 * layers, 8)),
        ],
        compiler_params=pltpu.CompilerParams(
            collective_id=0, has_side_effects=True, vmem_limit_bytes=64 * 1024 * 1024
        ),
    )(
        stream.reshape(rows * cols, width),
        gains,
        table,
        conv,
        w_qkv,
        w_out,
        w_up,
        w_down,
    )
    return result.reshape(rows, cols, width)


def solution(mesh):
    sizes = dict(mesh.shape)
    in_specs = (P("lat", "lon", None), P(), P(), P(), P(), P(), P(), P())
    return jax.shard_map(
        functools.partial(on_device, sizes["lat"], sizes["lon"]),
        mesh=mesh,
        in_specs=in_specs,
        out_specs=P("lat", "lon", None),
        check_vma=False,
    )
```

```python
import functools

import jax
import jax.numpy as jnp
from jax import lax
from jax.experimental import pallas as pl
from jax.experimental.pallas import tpu as pltpu
from jax.sharding import PartitionSpec as P

WINDOW = 7
REACH = 3
GROUP = 4
F32 = jnp.float32
BF16 = jnp.bfloat16

LEFT, RIGHT, TOP, BOTTOM, TOP_L, TOP_R, BOT_L, BOT_R = range(8)
STEPS = ((0, 1), (0, -1), (1, 0), (-1, 0), (1, 1), (1, -1), (-1, 1), (-1, -1))


def iota(shape, dim):
    return lax.broadcasted_iota(jnp.int32, shape, dim)


def hot(cond):
    return jnp.where(cond, 1.0, 0.0).astype(BF16)


def dot(a, b):
    return jnp.dot(a, b, preferred_element_type=F32)


def normed(wide, gain):
    scale = lax.rsqrt(jnp.mean(wide * wide, axis=-1, keepdims=True) + 1e-06)
    return (wide * scale * gain).astype(BF16)


def kernel(
    n_lat, n_lon, x_hbm, gains_hbm, table_hbm, conv_hbm, wqkv_hbm, wout_hbm, wup_hbm, wdown_hbm,
    out_ref, gains_ref, table, conv_ref, wqkv, wout, wup, wdown, kvb, near_l, near_r, xb, left, right, edge, lpad, pre, rows, spread,
    bias, row_bias, attn, in_sem, w_sem, send_sem, recv_sem,
):
    layers = wqkv.shape[0]
    tokens, width = x_hbm.shape
    cols = 16
    heads = table.shape[2]
    hid = wup.shape[2]
    lat = lax.axis_index("lat")
    lon = lax.axis_index("lon")
    has_up = lat > 0
    has_down = lat < n_lat - 1
    total_rows = n_lat * (tokens // cols)
    first_row = lat * (tokens // cols)

    loads = {}
    firsts = (("x", x_hbm, xb.at[0, pl.ds(64, 256)]), ("gains", gains_hbm, gains_ref), ("table", table_hbm, table), ("conv", conv_hbm, conv_ref))
    for k, (name, src, dst) in enumerate(firsts):
        loads[name] = pltpu.make_async_copy(src, dst, in_sem.at[k])
    loads["x"].start()
    loads["gains"].start()
    for n in range(layers):
        pairs = ((wqkv_hbm, wqkv), (wout_hbm, wout), (wup_hbm, wup), (wdown_hbm, wdown))
        for k, (src, dst) in enumerate(pairs):
            loads[n, k] = pltpu.make_async_copy(src.at[n], dst.at[n], w_sem.at[n, k])
            loads[n, k].start()
            if n == 0 and k == 0:
                loads["table"].start()
                loads["conv"].start()

    def target(step):
        return {"lat": lat + step[0], "lon": lax.rem(lon + step[1] + n_lon, n_lon)}

    def when_to(step, go):
        if step[0] == 0:
            go()
        else:
            pl.when(has_down if step[0] > 0 else has_up)(go)

    def when_from(step, go):
        when_to((-step[0], -step[1]), go)

    barrier = pltpu.get_barrier_semaphore()
    for step in STEPS:
        when_to(
            step,
            lambda step=step: pl.semaphore_signal(
                barrier, inc=1, device_id=target(step), device_id_type=pl.DeviceIdType.MESH
            ),
        )

    def remote(n, slot):
        own, lo, ro, ed = xb.at[n], left.at[n], right.at[n], edge.at[n]
        src, dst = (
            (ed.at[pl.ds(64, 64)], lo.at[pl.ds(16, 64)]),
            (ed.at[pl.ds(0, 64)], ro.at[pl.ds(16, 64)]),
            (own.at[pl.ds(256, 64)], own.at[pl.ds(0, 64)]),
            (own.at[pl.ds(64, 64)], own.at[pl.ds(320, 64)]),
            (ed.at[pl.ds(112, 16)], lo.at[pl.ds(0, 16)]),
            (ed.at[pl.ds(48, 16)], ro.at[pl.ds(0, 16)]),
            (ed.at[pl.ds(64, 16)], lo.at[pl.ds(80, 16)]),
            (ed.at[pl.ds(0, 16)], ro.at[pl.ds(80, 16)]),
        )[slot]
        return pltpu.make_async_remote_copy(
            src_ref=src,
            dst_ref=dst,
            send_sem=send_sem.at[n, slot],
            recv_sem=recv_sem.at[n, slot],
            device_id=target(STEPS[slot]),
            device_id_type=pl.DeviceIdType.MESH,
        )

    def send(n):
        for slot, step in enumerate(STEPS):
            when_to(step, lambda slot=slot: remote(n, slot).start())

    def receive(n):
        for slot, step in enumerate(STEPS):
            when_from(step, lambda slot=slot: remote(n, slot).wait_recv())

    @pl.when(jnp.logical_not(has_up))
    def _():
        for n in range(layers):
            xb[n, 0:64] = jnp.zeros((64, width), BF16)
            left[n, 0:16] = jnp.zeros((16, width), BF16)
            right[n, 0:16] = jnp.zeros((16, width), BF16)
        attn[320:352] = jnp.zeros((32, width), BF16)

    @pl.when(jnp.logical_not(has_down))
    def _():
        for n in range(layers):
            xb[n, 320:384] = jnp.zeros((64, width), BF16)
            left[n, 80:96] = jnp.zeros((16, width), BF16)
            right[n, 80:96] = jnp.zeros((16, width), BF16)
        attn[352:384] = jnp.zeros((32, width), BF16)

    lpad[0:16] = jnp.zeros((16, hid), F32)
    lpad[272:288] = jnp.zeros((16, hid), F32)

    m, t = iota((128, tokens), 0), iota((128, tokens), 1)
    pick_kv = hot(t == ((m & 63) >> 2) * cols + (m & 3) + jnp.where(m >= 64, cols - 4, 0))
    m, t = iota((128, 320), 0), iota((128, 320), 1)
    e = m & 31
    side = 4 * (4 * (m >> 4) + (m & 3) + 4)
    flank = jnp.where((m & 15) < 4, 128 + side + 3, jnp.where((m & 15) < 8, 224 + side, -1))
    above = jnp.where(e < 16, 48 + e, jnp.where(e == 16, 143, jnp.where(e == 17, 236, -1)))
    below = jnp.where(e < 16, 64 + e, jnp.where(e == 16, 211, jnp.where(e == 17, 304, -1)))
    pick_ring = hot(t == jnp.where(m < 64, flank, jnp.where(m < 96, above, below)))
    m, t = iota((32, 64), 0), iota((32, 64), 1)
    pick_side = hot(t == ((m & 15) >> 2) * 16 + (m & 3) + jnp.where(m < 16, 0, 4))
    t, k = iota((tokens, 64), 0), iota((tokens, 64), 1)
    place = hot(((k & 15) == (t >> 4)) & ((t & 15) == jnp.where(k < 32, 0, cols - 1)))
    head_of = iota((1, width), 1) >> 6
    head_hot = [hot(head_of == h) for h in range(heads)]

    def prepare(pick):
        for at in (0, 128):
            for b in range(WINDOW):
                spread[b, :, at : at + 128] = jnp.take_along_axis(
                    rows[b], pick[:, at : at + 128], axis=1
                )

    def chosen(row, offset):
        value = jnp.broadcast_to(spread[0, row : row + 1, :], offset.shape)
        for b in range(1, WINDOW):
            value = jnp.where(offset == b - REACH, spread[b, row : row + 1, :], value)
        return value

    def build_bias():
        for n in range(layers):
            for b in range(WINDOW):
                rows[b, heads * n : heads * (n + 1), 0 : 2 * WINDOW - 1] = table[n, b]
        x = iota((16, 256), 1)
        j = iota((16, 256), 0)
        own = x < 160
        on_left = x < 208
        y = jnp.where(on_left, x - 160, x - 208)
        p = jnp.where(own, x >> 4, (y >> 2) - 1)
        c = jnp.where(own, x & 15, jnp.where(on_left, (y & 3) - 4, (y & 3) + cols))
        col_ok = (c - j >= -REACH) & (c - j <= REACH)
        for i in range(GROUP):
            oks = []
            for group in (0, 1, 3):
                g = first_row + GROUP * group + i
                start = jnp.clip(g - REACH, 0, total_rows - WINDOW)
                r = first_row + GROUP * group - REACH + p
                oks.append(col_ok & (r >= start) & (r < start + WINDOW))
            prepare(jnp.clip(p[0:8] - i + REACH, 0, 2 * WINDOW - 2))
            for n in range(layers):
                for h in range(heads):
                    value = chosen(n * heads + h, c - j)
                    at = h * 80 + i * 16
                    for var in range(3):
                        bias[n, var, at : at + 16, :] = jnp.where(oks[var], value, -1000000000.0)
        e = iota((16, 256), 0)
        i, j = e & 3, jnp.where(e < 4, -1, cols)
        px, cx = p, c
        col_ok = (cx - j >= -REACH) & (cx - j <= REACH)
        oks = []
        for group in (0, 1, 3):
            g = first_row + GROUP * group + i
            start = jnp.clip(g - REACH, 0, total_rows - WINDOW)
            r = first_row + GROUP * group - REACH + px
            oks.append(col_ok & (r >= start) & (r < start + WINDOW))
        pick = jnp.clip(px - i + REACH, 0, 2 * WINDOW - 2)[0:8]
        for n in range(layers):
            for h in range(heads):
                value = jnp.zeros((8, 256), F32)
                for b in range(WINDOW):
                    source = jnp.broadcast_to(rows[b, n * heads + h : n * heads + h + 1, :], (8, 128))
                    got = [
                        jnp.take_along_axis(source, pick[:, at : at + 128], axis=1)
                        for at in (0, 128)
                    ]
                    value = jnp.where(
                        (cx - j)[0:8] == b - REACH, jnp.concatenate(got, axis=1), value
                    )
                at = h * 80 + 64
                for var in range(3):
                    bias[n, var, at : at + 8, :] = jnp.where(oks[var][0:8], value, -1000000000.0)
                    bias[n, var, at + 8 : at + 16, :] = jnp.zeros((8, 256), F32)
        x, e = iota((32, 256), 1), iota((32, 256), 0)
        j = jnp.where(e < 16, e, jnp.where(e == 16, -1, cols))
        own, on_left = x < 160, x < 208
        y = jnp.where(on_left, x - 160, x - 208)
        c = jnp.where(own, x & 15, jnp.where(on_left, (y & 3) - 4, (y & 3) + cols))
        for k, (here, first_own, first_near) in enumerate(((-1, -4, -4), (16, 10, 8))):
            away = jnp.where(own, first_own + (x >> 4), first_near + (y >> 2)) - here
            ok = (c - j >= -REACH) & (c - j <= REACH) & (away >= -REACH) & (away <= REACH)
            prepare(jnp.clip(away[0:8] + WINDOW - 1, 0, 2 * WINDOW - 2))
            for n in range(layers):
                for h in range(heads):
                    value = chosen(n * heads + h, c - j)
                    row_bias[n, k, h * 32 : h * 32 + 32, :] = jnp.where(ok, value, -1000000000.0)

    def attend(q, near, held, count):
        stacked = jnp.concatenate([q * head_hot[h] for h in range(heads)], axis=0)
        scores = lax.dot_general(
            stacked, near[:, :width], (((1,), (1,)), ((), ())), preferred_element_type=F32
        )
        scores = scores + held
        raised = jnp.exp(scores - jnp.max(scores, axis=-1, keepdims=True))
        weights = (raised * (1.0 / jnp.sum(raised, axis=-1, keepdims=True))).astype(BF16)
        mixed = dot(weights, near[:, width:])
        total = jnp.where(head_of == 0, mixed[0:count], 0.0)
        for h in range(1, heads):
            total = jnp.where(head_of == h, mixed[count * h : count * (h + 1)], total)
        return total.astype(BF16)

    def near_keys(own, side):
        parts = [kvb[own : own + 160, :], near_l[side : side + 48, :], near_r[side : side + 48, :]]
        return jnp.concatenate(parts, axis=0)

    scale = (width // heads) ** (-0.5)
    loads["x"].wait()
    for n in range(layers):
        current = xb[n, 64:320]
        edge[n] = dot(pick_kv, current).astype(BF16)
        if n == 0:
            count = 2 + jnp.where(has_up, 3, 0) + jnp.where(has_down, 3, 0)
            pl.semaphore_wait(barrier, count)
        send(n)
        if n == 0:
            loads["gains"].wait()
        gain = gains_ref[n, 0:1, :]
        wide = current.astype(F32)
        norm = normed(wide, gain)
        loads[n, 0].wait()
        kvb[64:320] = dot(norm, wqkv[n, :, width:]).astype(BF16)
        query = (dot(norm, wqkv[n, :, :width]).astype(BF16) * scale).astype(BF16)
        if n == 0:
            loads["table"].wait()
            build_bias()
            loads["conv"].wait()
        receive(n)
        around = jnp.concatenate([xb[n, 0:64], xb[n, 320:384], left[n], right[n]], axis=0)
        ring = dot(pick_ring, around)
        near = dot(normed(around.astype(F32), gain), wqkv[n, :, width:]).astype(BF16)
        kvb[0:64] = near[0:64]
        kvb[320:384] = near[64:128]
        near_l[...] = near[128:224]
        near_r[...] = near[224:320]
        ring_query = (dot(normed(ring, gain), wqkv[n, :, :width]).astype(BF16) * scale).astype(BF16)
        for group in range(4):
            at = 64 * group
            more = slice(16 * group, 16 * group + 16)
            q = jnp.concatenate([query[at : at + 64], ring_query[more]], axis=0)
            held = bias[n, (0, 1, 1, 2)[group]]
            got = attend(q, near_keys(at + 16, 16 * group), held, 80)
            attn[at : at + 64, :] = got[0:64]
            attn[256 + 16 * group : 272 + 16 * group, :] = got[64:80]

        @pl.when(has_up)
        def _():
            attn[320:352] = attend(ring_query[64:96], near_keys(0, 0), row_bias[n, 0], 32)

        @pl.when(has_down)
        def _():
            attn[352:384] = attend(ring_query[96:128], near_keys(224, 48), row_bias[n, 1], 32)

        loads[n, 1].wait()
        after = jnp.concatenate([wide, ring], axis=0) + dot(attn[...], wout[n])
        norm = normed(after, gains_ref[n, 1:2, :])
        after = after[0:tokens]
        loads[n, 2].wait()
        lift = dot(norm, wup[n]).astype(BF16)
        sides = dot(pick_side, lift[256:320])
        rims = lift[320:384].astype(F32)
        lpad[16:272] = lift[0:tokens].astype(F32)
        col = iota((tokens, 128), 0) & 15
        for ch in range(hid // 128):
            at = slice(128 * ch, 128 * ch + 128)
            above, here, below = lpad[0:256, at], lpad[16:272, at], lpad[32:288, at]

            def column(b):
                return (
                    conv_ref[0, b, n : n + 1, at] * above
                    + conv_ref[1, b, n : n + 1, at] * here
                    + conv_ref[2, b, n : n + 1, at] * below
                )

            pre[:, at] = (
                column(1)
                + jnp.where(col > 0, pltpu.roll(column(0), 1, 0), 0.0)
                + jnp.where(col < cols - 1, pltpu.roll(column(2), tokens - 1, 0), 0.0)
            )
        line = iota((16, hid), 0)

        def tap(a, b):
            return conv_ref[a, b, n : n + 1, :]

        def row_part(a, rim):
            middle = rim[0:16]
            back = jnp.where(line == 0, rim[16:17], pltpu.roll(middle, 1, 0))
            ahead = jnp.where(line == 15, rim[17:18], pltpu.roll(middle, 15, 0))
            return tap(a, 0) * back + tap(a, 1) * middle + tap(a, 2) * ahead

        def col_part(b, values):
            up = jnp.where(line == 0, 0.0, pltpu.roll(values, 1, 0))
            down = jnp.where(line == 15, 0.0, pltpu.roll(values, 15, 0))
            return tap(0, b) * up + tap(1, b) * values + tap(2, b) * down

        pieces = []
        for part in (col_part(0, sides[0:16]), col_part(2, sides[16:32])):
            high = part.astype(BF16)
            pieces += [high, (part - high.astype(F32)).astype(BF16)]
        pre[0:16] += row_part(0, rims[0:32])
        pre[240:256] += row_part(2, rims[32:64])
        whole = pre[...] + dot(place, jnp.concatenate(pieces, axis=0))
        hidden = jax.nn.gelu(whole, approximate=True).astype(BF16)
        loads[n, 3].wait()
        result = (after + dot(hidden, wdown[n])).astype(BF16)
        if n == layers - 1:
            out_ref[...] = result
        else:
            xb[n + 1, 64:320] = result

    for n in range(layers):
        for slot, step in enumerate(STEPS):
            when_to(step, lambda slot=slot: remote(n, slot).wait_send())


def on_device(n_lat, n_lon, stream, gains, w_qkv, table, w_out, w_up, conv, w_down):
    rows, cols, width = stream.shape
    layers, heads = table.shape[:2]
    table = table.transpose(0, 3, 1, 2)
    conv = conv.transpose(1, 2, 0, 3)
    hid = w_up.shape[2]
    vmem = pl.BlockSpec(memory_space=pltpu.VMEM)
    anywhere = pl.BlockSpec(memory_space=pltpu.HBM)
    result = pl.pallas_call(
        functools.partial(kernel, n_lat, n_lon),
        out_shape=jax.ShapeDtypeStruct((rows * cols, width), BF16),
        in_specs=[anywhere] * 8,
        out_specs=vmem,
        scratch_shapes=[
            pltpu.VMEM(gains.shape, F32),
            pltpu.VMEM(table.shape, F32),
            pltpu.VMEM(conv.shape, F32),
            pltpu.VMEM(w_qkv.shape, BF16),
            pltpu.VMEM(w_out.shape, BF16),
            pltpu.VMEM(w_up.shape, BF16),
            pltpu.VMEM(w_down.shape, BF16),
            pltpu.VMEM((384, 2 * width), BF16),
            pltpu.VMEM((96, 2 * width), BF16),
            pltpu.VMEM((96, 2 * width), BF16),
            pltpu.VMEM((layers, 384, width), BF16),
            pltpu.VMEM((layers, 96, width), BF16),
            pltpu.VMEM((layers, 96, width), BF16),
            pltpu.VMEM((layers, 128, width), BF16),
            pltpu.VMEM((288, hid), F32),
            pltpu.VMEM((256, hid), F32),
            pltpu.VMEM((WINDOW, layers * heads, 128), F32),
            pltpu.VMEM((WINDOW, layers * heads, 256), F32),
            pltpu.VMEM((layers, 3, 320, 256), F32),
            pltpu.VMEM((layers, 2, 128, 256), F32),
            pltpu.VMEM((384, width), BF16),
            pltpu.SemaphoreType.DMA((4,)),
            pltpu.SemaphoreType.DMA((layers, 4)),
            pltpu.SemaphoreType.DMA((layers, 8)),
            pltpu.SemaphoreType.DMA((layers, 8)),
        ],
        compiler_params=pltpu.CompilerParams(
            collective_id=0, has_side_effects=True, vmem_limit_bytes=64 * 1024 * 1024
        ),
    )(
        stream.reshape(rows * cols, width),
        gains,
        table,
        conv,
        w_qkv,
        w_out,
        w_up,
        w_down,
    )
    return result.reshape(rows, cols, width)


def solution(mesh):
    sizes = dict(mesh.shape)
    in_specs = (P("lat", "lon", None), P(), P(), P(), P(), P(), P(), P())
    return jax.shard_map(
        functools.partial(on_device, sizes["lat"], sizes["lon"]),
        mesh=mesh,
        in_specs=in_specs,
        out_specs=P("lat", "lon", None),
        check_vma=False,
    )
```

```python
import functools

import jax
import jax.numpy as jnp
from jax import lax
from jax.experimental import pallas as pl
from jax.experimental.pallas import tpu as pltpu
from jax.sharding import PartitionSpec as P

WINDOW = 7
REACH = 3
GROUP = 4
F32 = jnp.float32
BF16 = jnp.bfloat16

LEFT, RIGHT, TOP, BOTTOM, TOP_L, TOP_R, BOT_L, BOT_R = range(8)
STEPS = ((0, 1), (0, -1), (1, 0), (-1, 0), (1, 1), (1, -1), (-1, 1), (-1, -1))


def iota(shape, dim):
    return lax.broadcasted_iota(jnp.int32, shape, dim)


def hot(cond):
    return jnp.where(cond, 1.0, 0.0).astype(BF16)


def dot(a, b):
    return jnp.dot(a, b, preferred_element_type=F32)


def normed(wide, gain):
    scale = lax.rsqrt(jnp.mean(wide * wide, axis=-1, keepdims=True) + 1e-06)
    return (wide * scale * gain).astype(BF16)


def kernel(
    n_lat, n_lon, x_hbm, gains_hbm, table_hbm, conv_hbm, wqkv_hbm, wout_hbm, wup_hbm, wdown_hbm,
    out_ref, gains_ref, table, conv_ref, wqkv, wout, wup, wdown, kvb, near_l, near_r, xb, left, right, edge, lpad, pre, rows, spread,
    bias, row_bias, attn, in_sem, w_sem, send_sem, recv_sem,
):
    layers = wqkv.shape[0]
    tokens, width = x_hbm.shape
    cols = 16
    heads = table.shape[2]
    hid = wup.shape[2]
    lat = lax.axis_index("lat")
    lon = lax.axis_index("lon")
    has_up = lat > 0
    has_down = lat < n_lat - 1
    total_rows = n_lat * (tokens // cols)
    first_row = lat * (tokens // cols)

    loads = {}
    firsts = (("x", x_hbm, xb.at[0, pl.ds(64, 256)]), ("gains", gains_hbm, gains_ref), ("table", table_hbm, table), ("conv", conv_hbm, conv_ref))
    for k, (name, src, dst) in enumerate(firsts):
        loads[name] = pltpu.make_async_copy(src, dst, in_sem.at[k])
    loads["x"].start()
    loads["gains"].start()
    for n in range(layers):
        pairs = ((wqkv_hbm, wqkv), (wout_hbm, wout), (wup_hbm, wup), (wdown_hbm, wdown))
        for k, (src, dst) in enumerate(pairs):
            loads[n, k] = pltpu.make_async_copy(src.at[n], dst.at[n], w_sem.at[n, k])
            loads[n, k].start()
            if n == 0 and k == 0:
                loads["table"].start()
                loads["conv"].start()

    def target(step):
        return {"lat": lat + step[0], "lon": lax.rem(lon + step[1] + n_lon, n_lon)}

    def when_to(step, go):
        if step[0] == 0:
            go()
        else:
            pl.when(has_down if step[0] > 0 else has_up)(go)

    def when_from(step, go):
        when_to((-step[0], -step[1]), go)

    barrier = pltpu.get_barrier_semaphore()
    for step in STEPS:
        when_to(
            step,
            lambda step=step: pl.semaphore_signal(
                barrier, inc=1, device_id=target(step), device_id_type=pl.DeviceIdType.MESH
            ),
        )

    def remote(n, slot):
        own, lo, ro, ed = xb.at[n], left.at[n], right.at[n], edge.at[n]
        src, dst = (
            (ed.at[pl.ds(64, 64)], lo.at[pl.ds(16, 64)]),
            (ed.at[pl.ds(0, 64)], ro.at[pl.ds(16, 64)]),
            (own.at[pl.ds(256, 64)], own.at[pl.ds(0, 64)]),
            (own.at[pl.ds(64, 64)], own.at[pl.ds(320, 64)]),
            (ed.at[pl.ds(112, 16)], lo.at[pl.ds(0, 16)]),
            (ed.at[pl.ds(48, 16)], ro.at[pl.ds(0, 16)]),
            (ed.at[pl.ds(64, 16)], lo.at[pl.ds(80, 16)]),
            (ed.at[pl.ds(0, 16)], ro.at[pl.ds(80, 16)]),
        )[slot]
        return pltpu.make_async_remote_copy(
            src_ref=src,
            dst_ref=dst,
            send_sem=send_sem.at[n, slot],
            recv_sem=recv_sem.at[n, slot],
            device_id=target(STEPS[slot]),
            device_id_type=pl.DeviceIdType.MESH,
        )

    def send(n):
        for slot, step in enumerate(STEPS):
            when_to(step, lambda slot=slot: remote(n, slot).start())

    def receive(n):
        for slot, step in enumerate(STEPS):
            when_from(step, lambda slot=slot: remote(n, slot).wait_recv())

    @pl.when(jnp.logical_not(has_up))
    def _():
        for n in range(layers):
            xb[n, 0:64] = jnp.zeros((64, width), BF16)
            left[n, 0:16] = jnp.zeros((16, width), BF16)
            right[n, 0:16] = jnp.zeros((16, width), BF16)
        attn[320:352] = jnp.zeros((32, width), BF16)

    @pl.when(jnp.logical_not(has_down))
    def _():
        for n in range(layers):
            xb[n, 320:384] = jnp.zeros((64, width), BF16)
            left[n, 80:96] = jnp.zeros((16, width), BF16)
            right[n, 80:96] = jnp.zeros((16, width), BF16)
        attn[352:384] = jnp.zeros((32, width), BF16)

    lpad[0:16] = jnp.zeros((16, hid), F32)
    lpad[272:288] = jnp.zeros((16, hid), F32)

    m, t = iota((128, tokens), 0), iota((128, tokens), 1)
    pick_kv = hot(t == ((m & 63) >> 2) * cols + (m & 3) + jnp.where(m >= 64, cols - 4, 0))
    m, t = iota((128, 320), 0), iota((128, 320), 1)
    e = m & 31
    side = 4 * (4 * (m >> 4) + (m & 3) + 4)
    flank = jnp.where((m & 15) < 4, 128 + side + 3, jnp.where((m & 15) < 8, 224 + side, -1))
    above = jnp.where(e < 16, 48 + e, jnp.where(e == 16, 143, jnp.where(e == 17, 236, -1)))
    below = jnp.where(e < 16, 64 + e, jnp.where(e == 16, 211, jnp.where(e == 17, 304, -1)))
    pick_ring = hot(t == jnp.where(m < 64, flank, jnp.where(m < 96, above, below)))
    m, t = iota((32, 64), 0), iota((32, 64), 1)
    pick_side = hot(t == ((m & 15) >> 2) * 16 + (m & 3) + jnp.where(m < 16, 0, 4))
    t, k = iota((tokens, 64), 0), iota((tokens, 64), 1)
    place = hot(((k & 15) == (t >> 4)) & ((t & 15) == jnp.where(k < 32, 0, cols - 1)))
    head_of = iota((1, width), 1) >> 6
    head_hot = [hot(head_of == h) for h in range(heads)]

    def prepare(pick):
        for at in (0, 128):
            for b in range(WINDOW):
                spread[b, :, at : at + 128] = jnp.take_along_axis(
                    rows[b], pick[:, at : at + 128], axis=1
                )

    def chosen(row, offset):
        value = jnp.broadcast_to(spread[0, row : row + 1, :], offset.shape)
        for b in range(1, WINDOW):
            value = jnp.where(offset == b - REACH, spread[b, row : row + 1, :], value)
        return value

    def build_bias():
        for n in range(layers):
            for b in range(WINDOW):
                rows[b, heads * n : heads * (n + 1), 0 : 2 * WINDOW - 1] = table[n, b]
        x = iota((16, 256), 1)
        j = iota((16, 256), 0)
        own = x < 160
        on_left = x < 208
        y = jnp.where(on_left, x - 160, x - 208)
        p = jnp.where(own, x >> 4, (y >> 2) - 1)
        c = jnp.where(own, x & 15, jnp.where(on_left, (y & 3) - 4, (y & 3) + cols))
        col_ok = (c - j >= -REACH) & (c - j <= REACH)
        for i in range(GROUP):
            oks = []
            for group in (0, 1, 3):
                g = first_row + GROUP * group + i
                start = jnp.clip(g - REACH, 0, total_rows - WINDOW)
                r = first_row + GROUP * group - REACH + p
                oks.append(col_ok & (r >= start) & (r < start + WINDOW))
            prepare(jnp.clip(p[0:8] - i + REACH, 0, 2 * WINDOW - 2))
            for n in range(layers):
                for h in range(heads):
                    value = chosen(n * heads + h, c - j)
                    at = h * 80 + i * 16
                    for var in range(3):
                        bias[n, var, at : at + 16, :] = jnp.where(oks[var], value, -1000000000.0)
        e = iota((16, 256), 0)
        i, j = e & 3, jnp.where(e < 4, -1, cols)
        px, cx = p, c
        col_ok = (cx - j >= -REACH) & (cx - j <= REACH)
        oks = []
        for group in (0, 1, 3):
            g = first_row + GROUP * group + i
            start = jnp.clip(g - REACH, 0, total_rows - WINDOW)
            r = first_row + GROUP * group - REACH + px
            oks.append(col_ok & (r >= start) & (r < start + WINDOW))
        pick = jnp.clip(px - i + REACH, 0, 2 * WINDOW - 2)[0:8]
        for n in range(layers):
            for h in range(heads):
                value = jnp.zeros((8, 256), F32)
                for b in range(WINDOW):
                    source = jnp.broadcast_to(rows[b, n * heads + h : n * heads + h + 1, :], (8, 128))
                    got = [
                        jnp.take_along_axis(source, pick[:, at : at + 128], axis=1)
                        for at in (0, 128)
                    ]
                    value = jnp.where(
                        (cx - j)[0:8] == b - REACH, jnp.concatenate(got, axis=1), value
                    )
                at = h * 80 + 64
                for var in range(3):
                    bias[n, var, at : at + 8, :] = jnp.where(oks[var][0:8], value, -1000000000.0)
                    bias[n, var, at + 8 : at + 16, :] = jnp.zeros((8, 256), F32)
        x, e = iota((32, 256), 1), iota((32, 256), 0)
        j = jnp.where(e < 16, e, jnp.where(e == 16, -1, cols))
        own, on_left = x < 160, x < 208
        y = jnp.where(on_left, x - 160, x - 208)
        c = jnp.where(own, x & 15, jnp.where(on_left, (y & 3) - 4, (y & 3) + cols))
        for k, (here, first_own, first_near) in enumerate(((-1, -4, -4), (16, 10, 8))):
            away = jnp.where(own, first_own + (x >> 4), first_near + (y >> 2)) - here
            ok = (c - j >= -REACH) & (c - j <= REACH) & (away >= -REACH) & (away <= REACH)
            prepare(jnp.clip(away[0:8] + WINDOW - 1, 0, 2 * WINDOW - 2))
            for n in range(layers):
                for h in range(heads):
                    value = chosen(n * heads + h, c - j)
                    row_bias[n, k, h * 32 : h * 32 + 32, :] = jnp.where(ok, value, -1000000000.0)

    def attend(q, near, held, count):
        stacked = jnp.concatenate([q * head_hot[h] for h in range(heads)], axis=0)
        scores = lax.dot_general(
            stacked, near[:, :width], (((1,), (1,)), ((), ())), preferred_element_type=F32
        )
        scores = scores + held
        raised = jnp.exp(scores - jnp.max(scores, axis=-1, keepdims=True))
        weights = (raised * (1.0 / jnp.sum(raised, axis=-1, keepdims=True))).astype(BF16)
        mixed = dot(weights, near[:, width:])
        total = jnp.where(head_of == 0, mixed[0:count], 0.0)
        for h in range(1, heads):
            total = jnp.where(head_of == h, mixed[count * h : count * (h + 1)], total)
        return total.astype(BF16)

    def near_keys(own, side):
        parts = [kvb[own : own + 160, :], near_l[side : side + 48, :], near_r[side : side + 48, :]]
        return jnp.concatenate(parts, axis=0)

    scale = (width // heads) ** (-0.5)
    loads["x"].wait()
    for n in range(layers):
        current = xb[n, 64:320]
        edge[n] = dot(pick_kv, current).astype(BF16)
        if n == 0:
            count = 2 + jnp.where(has_up, 3, 0) + jnp.where(has_down, 3, 0)
            pl.semaphore_wait(barrier, count)
        send(n)
        if n == 0:
            loads["gains"].wait()
        gain = gains_ref[n, 0:1, :]
        wide = current.astype(F32)
        norm = normed(wide, gain)
        loads[n, 0].wait()
        kvb[64:320] = dot(norm, wqkv[n, :, width:]).astype(BF16)
        query = (dot(norm, wqkv[n, :, :width]).astype(BF16) * scale).astype(BF16)
        if n == 0:
            loads["table"].wait()
            build_bias()
            loads["conv"].wait()
        receive(n)
        around = jnp.concatenate([xb[n, 0:64], xb[n, 320:384], left[n], right[n]], axis=0)
        ring = dot(pick_ring, around)
        near = dot(normed(around.astype(F32), gain), wqkv[n, :, width:]).astype(BF16)
        kvb[0:64] = near[0:64]
        kvb[320:384] = near[64:128]
        near_l[...] = near[128:224]
        near_r[...] = near[224:320]
        ring_query = (dot(normed(ring, gain), wqkv[n, :, :width]).astype(BF16) * scale).astype(BF16)
        for group in range(4):
            at = 64 * group
            more = slice(16 * group, 16 * group + 16)
            q = jnp.concatenate([query[at : at + 64], ring_query[more]], axis=0)
            held = bias[n, (0, 1, 1, 2)[group]]
            got = attend(q, near_keys(at + 16, 16 * group), held, 80)
            attn[at : at + 64, :] = got[0:64]
            attn[256 + 16 * group : 272 + 16 * group, :] = got[64:80]

        @pl.when(has_up)
        def _():
            attn[320:352] = attend(ring_query[64:96], near_keys(0, 0), row_bias[n, 0], 32)

        @pl.when(has_down)
        def _():
            attn[352:384] = attend(ring_query[96:128], near_keys(224, 48), row_bias[n, 1], 32)

        loads[n, 1].wait()
        after = jnp.concatenate([wide, ring], axis=0) + dot(attn[...], wout[n])
        norm = normed(after, gains_ref[n, 1:2, :])
        after = after[0:tokens]
        loads[n, 2].wait()
        lift = dot(norm, wup[n]).astype(BF16)
        sides = dot(pick_side, lift[256:320])
        rims = lift[320:384].astype(F32)
        lpad[16:272] = lift[0:tokens].astype(F32)
        col = iota((tokens, 128), 0) & 15
        for ch in range(hid // 128):
            at = slice(128 * ch, 128 * ch + 128)
            above, here, below = lpad[0:256, at], lpad[16:272, at], lpad[32:288, at]

            def column(b):
                return (
                    conv_ref[0, b, n : n + 1, at] * above
                    + conv_ref[1, b, n : n + 1, at] * here
                    + conv_ref[2, b, n : n + 1, at] * below
                )

            pre[:, at] = (
                column(1)
                + jnp.where(col > 0, pltpu.roll(column(0), 1, 0), 0.0)
                + jnp.where(col < cols - 1, pltpu.roll(column(2), tokens - 1, 0), 0.0)
            )
        line = iota((16, hid), 0)

        def tap(a, b):
            return conv_ref[a, b, n : n + 1, :]

        def row_part(a, rim):
            middle = rim[0:16]
            back = jnp.where(line == 0, rim[16:17], pltpu.roll(middle, 1, 0))
            ahead = jnp.where(line == 15, rim[17:18], pltpu.roll(middle, 15, 0))
            return tap(a, 0) * back + tap(a, 1) * middle + tap(a, 2) * ahead

        def col_part(b, values):
            up = jnp.where(line == 0, 0.0, pltpu.roll(values, 1, 0))
            down = jnp.where(line == 15, 0.0, pltpu.roll(values, 15, 0))
            return tap(0, b) * up + tap(1, b) * values + tap(2, b) * down

        pieces = []
        for part in (col_part(0, sides[0:16]), col_part(2, sides[16:32])):
            high = part.astype(BF16)
            pieces += [high, (part - high.astype(F32)).astype(BF16)]
        pre[0:16] += row_part(0, rims[0:32])
        pre[240:256] += row_part(2, rims[32:64])
        whole = pre[...] + dot(place, jnp.concatenate(pieces, axis=0))
        hidden = jax.nn.gelu(whole, approximate=True).astype(BF16)
        loads[n, 3].wait()
        result = (after + dot(hidden, wdown[n])).astype(BF16)
        if n == layers - 1:
            out_ref[...] = result
        else:
            xb[n + 1, 64:320] = result

    for n in range(layers):
        for slot, step in enumerate(STEPS):
            when_to(step, lambda slot=slot: remote(n, slot).wait_send())


def on_device(n_lat, n_lon, stream, gains, w_qkv, table, w_out, w_up, conv, w_down):
    rows, cols, width = stream.shape
    layers, heads = table.shape[:2]
    table = table.transpose(0, 3, 1, 2)
    conv = conv.transpose(1, 2, 0, 3)
    hid = w_up.shape[2]
    vmem = pl.BlockSpec(memory_space=pltpu.VMEM)
    anywhere = pl.BlockSpec(memory_space=pltpu.HBM)
    result = pl.pallas_call(
        functools.partial(kernel, n_lat, n_lon),
        out_shape=pltpu.VMEM((rows * cols, width), BF16),
        in_specs=[anywhere] * 8,
        out_specs=vmem,
        scratch_shapes=[
            pltpu.VMEM(gains.shape, F32),
            pltpu.VMEM(table.shape, F32),
            pltpu.VMEM(conv.shape, F32),
            pltpu.VMEM(w_qkv.shape, BF16),
            pltpu.VMEM(w_out.shape, BF16),
            pltpu.VMEM(w_up.shape, BF16),
            pltpu.VMEM(w_down.shape, BF16),
            pltpu.VMEM((384, 2 * width), BF16),
            pltpu.VMEM((96, 2 * width), BF16),
            pltpu.VMEM((96, 2 * width), BF16),
            pltpu.VMEM((layers, 384, width), BF16),
            pltpu.VMEM((layers, 96, width), BF16),
            pltpu.VMEM((layers, 96, width), BF16),
            pltpu.VMEM((layers, 128, width), BF16),
            pltpu.VMEM((288, hid), F32),
            pltpu.VMEM((256, hid), F32),
            pltpu.VMEM((WINDOW, layers * heads, 128), F32),
            pltpu.VMEM((WINDOW, layers * heads, 256), F32),
            pltpu.VMEM((layers, 3, 320, 256), F32),
            pltpu.VMEM((layers, 2, 128, 256), F32),
            pltpu.VMEM((384, width), BF16),
            pltpu.SemaphoreType.DMA((4,)),
            pltpu.SemaphoreType.DMA((layers, 4)),
            pltpu.SemaphoreType.DMA((layers, 8)),
            pltpu.SemaphoreType.DMA((layers, 8)),
        ],
        compiler_params=pltpu.CompilerParams(
            collective_id=0, has_side_effects=True, vmem_limit_bytes=58 * 1024 * 1024
        ),
    )(
        stream.reshape(rows * cols, width),
        gains,
        table,
        conv,
        w_qkv,
        w_out,
        w_up,
        w_down,
    )
    return result.reshape(rows, cols, width)


def solution(mesh):
    sizes = dict(mesh.shape)
    in_specs = (P("lat", "lon", None), P(), P(), P(), P(), P(), P(), P())
    return jax.shard_map(
        functools.partial(on_device, sizes["lat"], sizes["lon"]),
        mesh=mesh,
        in_specs=in_specs,
        out_specs=P("lat", "lon", None),
        check_vma=False,
    )
```
